1024 devices in a mesh: seq: 128 (over x_lo, z, core), chan: 8 (over y, x_hi).
Axes of the slice: x: 4 (x_hi: 2, x_lo: 2; x = x_hi * 2 + x_lo), y: 4, z: 32, core: 2. Of those that a mesh axis runs over, the one named last changes fastest.
Arguments:
- grad_out: bfloat16 [16384, 4096], P('seq', 'chan'), may hold values from -6 to 6
- out_weight: bfloat16 [4096, 4096], P('seq', 'chan'), may hold values from -0.09375 to 0.09375
- gate_stream: bfloat16 [4096, 16384], P('chan', 'seq'), may hold values from -6 to 6
- conv_output: bfloat16 [4096, 16384], P('chan', 'seq'), may hold values from -6 to 6
- key_stream: bfloat16 [4096, 16384], P('chan', 'seq'), may hold values from -6 to 6
- value_stream: bfloat16 [4096, 16384], P('chan', 'seq'), may hold values from -6 to 6
- long_filter: bfloat16 [4096, 16384], P(('chan', 'seq')), may hold values from 0 to 1
Outputs:
- grad_gate: bfloat16 [4096, 16384], P('chan', 'seq')
- grad_key: bfloat16 [4096, 16384], P('chan', 'seq')
- grad_value: bfloat16 [4096, 16384], P('chan', 'seq')
The draws below stay inside these ranges and needn't reach their ends.
All inputs are finite; a program needn't handle non-finite values.
Results may differ from the reference program's by a relative error of at most 0.007.
Values may be sent and summed in bfloat16 or wider, within the bound.
A program may use at most 64 MiB of HBM per device.

```python
import math
import jax
import jax.numpy as jnp
from jax import lax

FEATURES = 4096
CONV_CHANNELS = 4096
SEQUENCE_LENGTH = 16384


def draw_long_filter(key, part):
    random_keys = jax.random.split(key, 6)
    delay_index = jnp.arange(SEQUENCE_LENGTH, dtype=jnp.int32)[None, :]
    slow_share = 0.5
    slow_pick = jax.random.uniform(random_keys[0], (CONV_CHANNELS, 1), jnp.float32)
    slow_rate = jnp.exp(jax.random.uniform(random_keys[1], (CONV_CHANNELS, 1), jnp.float32, math.log(0.05 / SEQUENCE_LENGTH), math.log(2.0 / SEQUENCE_LENGTH)))
    fast_rate = jnp.exp(jax.random.uniform(random_keys[2], (CONV_CHANNELS, 1), jnp.float32, math.log(2.0 / SEQUENCE_LENGTH), math.log(1.0 / 30.0)))
    falloff_speed = jnp.where(slow_pick < slow_share, slow_rate, fast_rate)
    jitter_level = 0.5 + jax.random.uniform(random_keys[3], (CONV_CHANNELS, SEQUENCE_LENGTH), jnp.float32)
    spike_delay = jax.random.randint(random_keys[4], (CONV_CHANNELS, 3), 0, SEQUENCE_LENGTH, jnp.int32)
    spike_retain = jax.random.uniform(random_keys[5], (CONV_CHANNELS, 3), jnp.float32, 0.5, 0.8)
    spike_factor = jnp.ones((CONV_CHANNELS, SEQUENCE_LENGTH), jnp.float32)
    for spike_index in range(3):
        elapsed_steps = delay_index >= spike_delay[:, spike_index:spike_index + 1]
        spike_factor = spike_factor * jnp.where(elapsed_steps, spike_retain[:, spike_index:spike_index + 1], 1.0)
    filter_magnitude = jnp.sqrt(2.0 * falloff_speed + 1.0 / SEQUENCE_LENGTH)
    filter_coefficients = filter_magnitude * jnp.exp(-falloff_speed * delay_index.astype(jnp.float32)) * jitter_level * spike_factor
    return filter_coefficients.astype(jnp.bfloat16)


def levels(key, shape, shards, smallest, largest):
    def one(axis_at, blocks):
        draws = jax.random.uniform(jax.random.fold_in(jax.random.fold_in(key, 6), axis_at), (blocks,), jnp.float32, smallest / len(shards), largest / len(shards))
        return jnp.repeat(jnp.exp(draws), shape[axis_at] // blocks).reshape((-1,) + (1,) * (len(shape) - axis_at - 1))

    loudness = one(*shards[0])
    for cut in shards[1:]:
        loudness = loudness * one(*cut)
    return loudness


def scatter_about(rng, shape, spread, limit, cuts=(), kind=jnp.bfloat16):
    level = levels(rng, shape, cuts, -0.22, 0.18) if cuts else 1.0
    entries = jax.random.normal(rng, shape, jnp.float32) * spread * level
    return jnp.minimum(jnp.maximum(entries, -limit), limit).astype(kind)


def setup_inputs(seed: int = 0) -> dict:
    arg_keys = jax.random.split(jax.random.key(seed), 8)
    grad_out = scatter_about(arg_keys[0], (SEQUENCE_LENGTH, FEATURES), 1.0, 6.0, ((0, 128), (1, 8)))
    out_weight = scatter_about(arg_keys[1], (FEATURES, CONV_CHANNELS), FEATURES ** -0.5, 0.09375, ((0, 128), (1, 8)))
    gate_stream = scatter_about(arg_keys[2], (CONV_CHANNELS, SEQUENCE_LENGTH), 1.0, 6.0, ((0, 8), (1, 128)))
    conv_output = scatter_about(arg_keys[3], (CONV_CHANNELS, SEQUENCE_LENGTH), 1.0, 6.0, ((0, 8), (1, 128)))
    key_stream = scatter_about(arg_keys[4], (CONV_CHANNELS, SEQUENCE_LENGTH), 1.0, 6.0, ((0, 8), (1, 128)))
    value_stream = scatter_about(arg_keys[5], (CONV_CHANNELS, SEQUENCE_LENGTH), 1.0, 6.0, ((0, 8), (1, 128)))
    long_filter = draw_long_filter(jax.random.fold_in(arg_keys[7], 71), 0)
    return {"grad_out": grad_out, "out_weight": out_weight, "gate_stream": gate_stream, "conv_output": conv_output, "key_stream": key_stream, "value_stream": value_stream, "long_filter": long_filter}


def correlate(gated_grad, filter_coefficients):
    seq_len = gated_grad.shape[1]
    block_count = gated_grad.shape[0] // 64

    def block_corr(pair_input):
        signal, kernel = pair_input
        spec_signal = jnp.fft.rfft(signal, 2 * seq_len, axis=-1)
        spec_kernel = jnp.fft.rfft(kernel, 2 * seq_len, axis=-1)
        joined = jnp.conj(spec_kernel) * spec_signal
        return jnp.fft.irfft(joined, 2 * seq_len, axis=-1)[:, :seq_len]

    result = lax.map(block_corr, (gated_grad.reshape(block_count, 64, seq_len), filter_coefficients.reshape(block_count, 64, seq_len)))
    return result.reshape(-1, seq_len)


def reference(grad_out, out_weight, gate_stream, conv_output, key_stream, value_stream, long_filter):
    grad_mix = jnp.dot(out_weight.astype(jnp.float32).T, grad_out.astype(jnp.float32).T, precision=lax.Precision.HIGHEST)
    grad_gate = (grad_mix * conv_output.astype(jnp.float32)).astype(jnp.bfloat16)
    gated_grad = (grad_mix * gate_stream.astype(jnp.float32)).astype(jnp.bfloat16)
    gated_grad = lax.optimization_barrier(gated_grad)
    corr_full = correlate(gated_grad.astype(jnp.float32), long_filter.astype(jnp.float32))
    grad_inner = lax.optimization_barrier(corr_full.astype(jnp.bfloat16))
    inner_wide = grad_inner.astype(jnp.float32)
    grad_key = (inner_wide * value_stream.astype(jnp.float32)).astype(jnp.bfloat16)
    grad_value = (inner_wide * key_stream.astype(jnp.float32)).astype(jnp.bfloat16)
    return (grad_gate, grad_key, grad_value)
```

```python
import functools
import math

import jax
import jax.numpy as jnp
import numpy as np
from jax import lax
from jax.experimental import pallas as pl
from jax.experimental.pallas import tpu as pltpu
from jax.sharding import PartitionSpec as P

MESH = pl.DeviceIdType.MESH
ZN = 32
CHAN = 8
VMEM = pltpu.VMEM


def seq_index(x, z, core):
    return (x * ZN + z) * 2 + core


def my_place():
    me = lax.axis_index("seq")
    return me, me // (2 * ZN), lax.rem(me // 2, ZN), lax.rem(me, 2)


def gather_kernel(g_ref, w_ref, gate_ref, conv_ref, gg_ref, gated_ref, wf, gf, acc,
                  recv_r, recv_l, recv_x, recv_p, recv_q, recv_g, send_w, send_q, send_g, local):
    me, x, z, core = my_place()
    chan = lax.axis_index("chan")
    zr, zl = lax.rem(z + 1, ZN), lax.rem(z + ZN - 1, ZN)
    right, left = seq_index(x, zr, core), seq_index(x, zl, core)
    partner, across = seq_index(x, z, 1 - core), seq_index(1 - x, z, core)

    barrier = pltpu.get_barrier_semaphore()
    for peer in (right, left, partner, across):
        pl.semaphore_signal(barrier, inc=1, device_id={"seq": peer}, device_id_type=MESH)
    for step in range(1, CHAN):
        pl.semaphore_signal(barrier, inc=1, device_id={"chan": lax.rem(chan + step, CHAN)}, device_id_type=MESH)
    own_w = pltpu.make_async_copy(w_ref, wf.at[x, z, core], local.at[0])
    own_w.start()
    own_g = pltpu.make_async_copy(g_ref, gf.at[chan], local.at[1])
    own_g.start()
    pl.semaphore_wait(barrier, 4 + CHAN - 1)

    def send(src, slot_z, target, send_sem, recv_sem):
        pltpu.make_async_remote_copy(
            src_ref=src, dst_ref=wf.at[x, slot_z, core], send_sem=send_sem, recv_sem=recv_sem,
            device_id={"seq": target}, device_id_type=MESH,
        ).start()

    send(w_ref, z, right, send_w, recv_r.at[0])
    send(w_ref, z, left, send_w, recv_l.at[0])
    send(w_ref, z, across, send_w, recv_x)
    send(w_ref, z, partner, send_w, recv_p)
    for step in range(1, CHAN):
        pltpu.make_async_remote_copy(
            src_ref=g_ref, dst_ref=gf.at[chan], send_sem=send_g, recv_sem=recv_g,
            device_id={"chan": lax.rem(chan + step, CHAN)}, device_id_type=MESH,
        ).start()

    def arrived(slot_z, sem):
        here = wf.at[x, slot_z, core]
        pltpu.make_async_copy(here, here, sem).wait()
        return here

    def hop(k, _):
        from_left, from_right = lax.rem(z + 2 * ZN - 1 - k, ZN), lax.rem(z + 1 + k, ZN)
        shard = arrived(from_left, recv_r.at[k])
        send(shard, from_left, right, send_w, recv_r.at[k + 1])
        other = arrived(from_right, recv_l.at[k])

        @pl.when(k < 14)
        def _():
            send(other, from_right, left, send_w, recv_l.at[k + 1])

        send(shard, from_left, across, send_w, recv_x)
        send(other, from_right, across, send_w, recv_x)
        send(shard, from_left, partner, send_w, recv_p)
        send(other, from_right, partner, send_w, recv_p)
        return 0

    lax.fori_loop(0, 15, hop, 0)
    last = lax.rem(z + 16, ZN)
    shard = arrived(last, recv_r.at[15])
    send(shard, last, across, send_w, recv_x)
    send(shard, last, partner, send_w, recv_p)

    quarter = wf.at[1 - x, :, core]
    pltpu.make_async_copy(quarter, quarter, recv_x).wait()
    pltpu.make_async_remote_copy(
        src_ref=quarter, dst_ref=quarter, send_sem=send_q, recv_sem=recv_q,
        device_id={"seq": partner}, device_id_type=MESH,
    ).start()

    own_w.wait()
    own_g.wait()
    others = gf.at[pl.ds(0, CHAN - 1)]
    pltpu.make_async_copy(others, others, recv_g).wait()
    theirs = wf.at[x, :, 1 - core]
    pltpu.make_async_copy(theirs, theirs, recv_p).wait()
    diagonal = wf.at[1 - x, :, 1 - core]
    pltpu.make_async_copy(diagonal, diagonal, recv_q).wait()

    acc[...] = jnp.zeros_like(acc)

    def multiply(j, _):
        block = wf[j // 4, pl.ds(lax.rem(j, 4) * 8, 8)].reshape(512, 512)
        acc[...] += jnp.dot(gf[j], block, preferred_element_type=jnp.float32)
        return 0

    lax.fori_loop(0, CHAN, multiply, 0)
    mix = acc[...].T
    gg_ref[...] = (mix * conv_ref[...].astype(jnp.float32)).astype(jnp.bfloat16)
    gated_ref[...] = (mix * gate_ref[...].astype(jnp.float32)).astype(jnp.bfloat16)

    pltpu.make_async_copy(quarter, quarter, send_q).wait()
    pltpu.make_async_copy(others, others, send_g).wait()
    for amount in (quarter, quarter):
        pltpu.make_async_copy(amount, amount, send_w).wait()
    rest = wf.at[x, pl.ds(0, 31), core]
    pltpu.make_async_copy(rest, rest, send_w).wait()


def gather_multiply(grad_out, out_weight, gate_stream, conv_output):
    space = pl.BlockSpec(memory_space=VMEM)
    dma = pltpu.SemaphoreType.DMA
    out = jax.ShapeDtypeStruct((512, 128), jnp.bfloat16)
    return pl.pallas_call(
        gather_kernel,
        out_shape=(out, out),
        in_specs=[space] * 4,
        out_specs=(space, space),
        scratch_shapes=[
            VMEM((2, ZN, 2, 32, 512), jnp.bfloat16),
            VMEM((CHAN, 128, 512), jnp.bfloat16),
            VMEM((128, 512), jnp.float32),
            dma((16,)), dma((16,)), dma, dma, dma, dma, dma, dma, dma, dma((2,)),
        ],
        compiler_params=pltpu.CompilerParams(collective_id=0, has_side_effects=True, vmem_limit_bytes=32 << 20),
        name="gather_multiply",
    )(grad_out, out_weight, gate_stream, conv_output)


def exchange_kernel(x_ref, o_ref, barrier_unused, recv, sent, local):
    me, x, z, core = my_place()

    def peers(act):
        def body(m, _):
            k = (m + 1) // 2
            away = 16 - k
            there = lax.rem(z + ZN + away * (2 * lax.rem(m, 2) - 1), ZN)
            for flip_x, flip_core in ((1, 0), (1, 1), (0, 0), (0, 1)):
                other_x = x + flip_x * (1 - 2 * x)
                other_core = core + flip_core * (1 - 2 * core)
                if flip_x == 0 and flip_core == 0:
                    @pl.when(m < ZN - 1)
                    def _():
                        act(seq_index(other_x, there, other_core))
                else:
                    act(seq_index(other_x, there, other_core))
            return 0

        lax.fori_loop(0, ZN, body, 0)

    barrier = pltpu.get_barrier_semaphore()
    peers(lambda peer: pl.semaphore_signal(barrier, inc=1, device_id={"seq": peer}, device_id_type=MESH))
    own = pltpu.make_async_copy(x_ref.at[me], o_ref.at[me], local)
    own.start()
    pl.semaphore_wait(barrier, 127)
    peers(lambda peer: pltpu.make_async_remote_copy(
        src_ref=x_ref.at[peer], dst_ref=o_ref.at[me], send_sem=sent, recv_sem=recv,
        device_id={"seq": peer}, device_id_type=MESH).start())
    own.wait()
    most = o_ref.at[pl.ds(0, 127)]
    pltpu.make_async_copy(most, most, recv).wait()
    pltpu.make_async_copy(most, most, sent).wait()


def exchange(blocks):
    space = pl.BlockSpec(memory_space=VMEM)
    dma = pltpu.SemaphoreType.DMA
    return pl.pallas_call(
        exchange_kernel,
        out_shape=jax.ShapeDtypeStruct(blocks.shape, blocks.dtype),
        in_specs=[space],
        out_specs=space,
        scratch_shapes=[pltpu.SemaphoreType.REGULAR, dma, dma, dma],
        compiler_params=pltpu.CompilerParams(collective_id=1, has_side_effects=True),
        name="exchange",
    )(blocks)


def tables(outer, inner):
    total = outer * inner
    def angles(a, b, n):
        return 2.0 * np.pi * ((np.arange(a)[:, None] * np.arange(b)[None, :]) % n) / n
    out = angles(outer, outer, outer)
    inn = angles(inner, inner, inner)
    twist = angles(outer, inner, total)
    f = np.float32
    return tuple(v.astype(f) for v in (np.cos(out), -np.sin(out), np.cos(inn), -np.sin(inn), np.cos(twist), -np.sin(twist)))


def outer_exact(table, signal):
    high = jnp.asarray(table).astype(jnp.bfloat16)
    low = (jnp.asarray(table) - high.astype(jnp.float32)).astype(jnp.bfloat16)
    first = jnp.einsum("ab,cbk->cak", high, signal, preferred_element_type=jnp.float32)
    return first + jnp.einsum("ab,cbk->cak", low, signal, preferred_element_type=jnp.float32)


def wide(spec, a, b):
    return jnp.einsum(spec, a, b, precision=lax.Precision.HIGH, preferred_element_type=jnp.float32)


def correlate(blocks, filters):
    channels = blocks.shape[1]
    oc, os_, ic, is_, tc, ts = tables(256, 128)
    both = jnp.concatenate([jnp.swapaxes(blocks, 0, 1), filters], axis=0)
    p_re = outer_exact(oc[:, :128], both)
    p_im = outer_exact(os_[:, :128], both)
    t_re = p_re * tc - p_im * ts
    t_im = p_re * ts + p_im * tc
    inner = "cak,kl->cal"
    s_re = wide(inner, t_re, ic) - wide(inner, t_im, is_)
    s_im = wide(inner, t_re, is_) + wide(inner, t_im, ic)
    a_re, k_re = s_re[:channels], s_re[channels:]
    a_im, k_im = s_im[:channels], s_im[channels:]
    j_re = k_re * a_re + k_im * a_im
    j_im = k_re * a_im - k_im * a_re
    b_re = wide(inner, j_re, ic) + wide(inner, j_im, is_)
    b_im = wide(inner, j_im, ic) - wide(inner, j_re, is_)
    v_re = b_re * tc + b_im * ts
    v_im = b_im * tc - b_re * ts
    outer = "ab,cbk->cak"
    full = (wide(outer, oc[:128], v_re) + wide(outer, os_[:128], v_im)) / (256 * 128)
    return jnp.swapaxes(full.astype(jnp.bfloat16), 0, 1)


def per_device(grad_out, out_weight, gate_stream, conv_output, key_stream, value_stream, long_filter):
    grad_gate, gated = gather_multiply(grad_out, out_weight, gate_stream, conv_output)
    blocks = exchange(gated.reshape(128, 4, 128))
    inner = correlate(blocks, long_filter.reshape(4, 128, 128))
    grad_inner = exchange(inner).reshape(512, 128).astype(jnp.float32)
    grad_key = (grad_inner * value_stream.astype(jnp.float32)).astype(jnp.bfloat16)
    grad_value = (grad_inner * key_stream.astype(jnp.float32)).astype(jnp.bfloat16)
    return (grad_gate, grad_key, grad_value)


def solution(mesh):
    in_specs = (
        P("seq", "chan"), P("seq", "chan"), P("chan", "seq"), P("chan", "seq"),
        P("chan", "seq"), P("chan", "seq"), P(("chan", "seq"), None),
    )
    out_specs = (P("chan", "seq"), P("chan", "seq"), P("chan", "seq"))
    return jax.shard_map(per_device, mesh=mesh, in_specs=in_specs, out_specs=out_specs, check_vma=False)
```

```python
import jax
import jax.numpy as jnp
import ml_dtypes
import numpy as np
from jax import lax
from jax.experimental import pallas as pl
from jax.experimental.pallas import tpu as pltpu
from jax.sharding import PartitionSpec as P

MESH = pl.DeviceIdType.MESH
VMEM = pltpu.VMEM
F32 = jnp.float32
BF16 = jnp.bfloat16
ZN = 32
CHAN = 8
SEQ = 128
CH = 4
ROWS = 144
WIDTH = SEQ * CH


def seq_index(x, z, core):
    return (x * ZN + z) * 2 + core


def split(values):
    high = values.astype(BF16)
    return high, (values - high.astype(F32)).astype(BF16)


def dot(a, b):
    return jnp.dot(a, b, preferred_element_type=F32)


def wide_dot(values, high, low):
    a, b = split(values)
    return dot(a, high) + (dot(b, high) + dot(a, low))


def dot_wide(high, low, values):
    a, b = split(values)
    return dot(high, a) + (dot(high, b) + dot(low, a))


def kernel(g_hbm, w_hbm, gate_hbm, conv_hbm, key_hbm, value_hbm, filt_hbm,
           t1h_hbm, t1l_hbm, twc_hbm, tws_hbm, t2h_hbm, t2l_hbm, t4h_hbm, t4l_hbm,
           gg_ref, gk_ref, gv_ref,
           wf, gf, acc, gate, conv, key, value, filt,
           t1h, t1l, twc, tws, t2h, t2l, t4h, t4l,
           perm, back, turned, spec, out1, in1, out2, in2,
           recv_r, recv_l, recv_x, recv_p, recv_q, recv_gx, recv_gy, send_w, send_q, send_g,
           recv_1, sent_1, recv_2, sent_2, local, loads):
    me = lax.axis_index("seq")
    chan = lax.axis_index("chan")
    x, z, core = me // (2 * ZN), lax.rem(me // 2, ZN), lax.rem(me, 2)
    zr, zl = lax.rem(z + 1, ZN), lax.rem(z + ZN - 1, ZN)
    right, left = seq_index(x, zr, core), seq_index(x, zl, core)
    partner, across = seq_index(x, z, 1 - core), seq_index(1 - x, z, core)
    y, x_hi = chan // 2, lax.rem(chan, 2)
    opposite = y * 2 + 1 - x_hi
    rows = [lax.rem(y + step, 4) * 2 + x_hi for step in (1, 3, 2)]

    barrier = pltpu.get_barrier_semaphore()
    for peer in (right, left, partner, across):
        pl.semaphore_signal(barrier, inc=1, device_id={"seq": peer}, device_id_type=MESH)
    for peer in (opposite, *rows):
        pl.semaphore_signal(barrier, inc=1, device_id={"chan": peer}, device_id_type=MESH)
    own_w = pltpu.make_async_copy(w_hbm, wf.at[x, z, core], local.at[0])
    own_g = pltpu.make_async_copy(g_hbm, gf.at[chan], local.at[1])
    own_w.start()
    own_g.start()
    early = [(filt_hbm, filt), (t1h_hbm, t1h), (t1l_hbm, t1l), (twc_hbm, twc), (tws_hbm, tws), (t2h_hbm, t2h), (t2l_hbm, t2l)]
    late = [(gate_hbm, gate), (conv_hbm, conv), (key_hbm, key), (value_hbm, value), (t4h_hbm, t4h), (t4l_hbm, t4l)]
    pulls = [pltpu.make_async_copy(src, dst, loads.at[n]) for n, (src, dst) in enumerate(early + late)]
    for pull in pulls:
        pull.start()
    pl.semaphore_wait(barrier, 8)

    def send(src, slot_z, target, recv_sem):
        pltpu.make_async_remote_copy(
            src_ref=src, dst_ref=wf.at[x, slot_z, core], send_sem=send_w, recv_sem=recv_sem,
            device_id={"seq": target}, device_id_type=MESH,
        ).start()

    def send_g_to(src, slot, target, recv_sem):
        pltpu.make_async_remote_copy(
            src_ref=src, dst_ref=gf.at[slot], send_sem=send_g, recv_sem=recv_sem,
            device_id={"chan": target}, device_id_type=MESH,
        ).start()

    send(w_hbm, z, right, recv_r.at[0])
    send(w_hbm, z, left, recv_l.at[0])
    send(w_hbm, z, across, recv_x)
    send(w_hbm, z, partner, recv_p)
    send_g_to(g_hbm, chan, opposite, recv_gx)
    for peer in rows:
        send_g_to(g_hbm, chan, peer, recv_gy)

    def arrived(here, sem):
        pltpu.make_async_copy(here, here, sem).wait()

    def outer_inner(blocks):
        beside = jnp.concatenate([blocks[c * SEQ:(c + 1) * SEQ] for c in range(CH)], axis=1)
        part = dot(t1h[...], beside) + dot(t1l[...], beside)
        for c in range(CH):
            re, im = part[:ROWS, c * SEQ:(c + 1) * SEQ], part[ROWS:, c * SEQ:(c + 1) * SEQ]
            turned[c * ROWS:(c + 1) * ROWS, :SEQ] = re * twc[...] - im * tws[...]
            turned[c * ROWS:(c + 1) * ROWS, SEQ:] = re * tws[...] + im * twc[...]

    def hop(k, _):
        from_left, from_right = lax.rem(z + 2 * ZN - 1 - k, ZN), lax.rem(z + 1 + k, ZN)
        shard, other = wf.at[x, from_left, core], wf.at[x, from_right, core]
        arrived(shard, recv_r.at[k])
        send(shard, from_left, right, recv_r.at[k + 1])
        arrived(other, recv_l.at[k])

        @pl.when(k < 14)
        def _():
            send(other, from_right, left, recv_l.at[k + 1])

        send(shard, from_left, across, recv_x)
        send(other, from_right, across, recv_x)
        send(shard, from_left, partner, recv_p)
        send(other, from_right, partner, recv_p)

        @pl.when(k == 3)
        def _():
            arrived(gf.at[opposite], recv_gx)
            for peer in rows:
                send_g_to(gf.at[opposite], opposite, peer, recv_gy)

        @pl.when(k == 4)
        def _():
            row = lax.broadcasted_iota(jnp.int32, (WIDTH, WIDTH), 0)
            col = lax.broadcasted_iota(jnp.int32, (WIDTH, WIDTH), 1)
            perm[...] = jnp.where(col == (row % SEQ) * CH + row // SEQ, 1.0, 0.0).astype(BF16)
            for pull in pulls[:len(early)]:
                pull.wait()

        @pl.when(k == 5)
        def _():
            row = lax.broadcasted_iota(jnp.int32, (WIDTH, WIDTH), 0)
            col = lax.broadcasted_iota(jnp.int32, (WIDTH, WIDTH), 1)
            back[...] = jnp.where(col == (row % CH) * SEQ + row // CH, 1.0, 0.0).astype(BF16)

        @pl.when(k == 6)
        def _():
            outer_inner(dot(perm[...], filt.reshape(WIDTH, SEQ)[...]).astype(BF16))

        @pl.when(k == 8)
        def _():
            spec[...] = wide_dot(turned[...], t2h[...], t2l[...])

        return 0

    lax.fori_loop(0, 15, hop, 0)
    last = lax.rem(z + 16, ZN)
    shard = wf.at[x, last, core]
    arrived(shard, recv_r.at[15])
    send(shard, last, across, recv_x)
    send(shard, last, partner, recv_p)

    quarter = wf.at[1 - x, :, core]
    arrived(quarter, recv_x)
    pltpu.make_async_remote_copy(
        src_ref=quarter, dst_ref=quarter, send_sem=send_q, recv_sem=recv_q,
        device_id={"seq": partner}, device_id_type=MESH,
    ).start()

    own_w.wait()
    own_g.wait()
    for pull in pulls[len(early):]:
        pull.wait()
    arrived(gf.at[pl.ds(0, 6)], recv_gy)
    arrived(wf.at[x, :, 1 - core], recv_p)
    arrived(wf.at[1 - x, :, 1 - core], recv_q)

    acc[...] = jnp.zeros_like(acc)

    def multiply(j, _):
        block = wf[j // 4, pl.ds(lax.rem(j, 4) * 8, 8)].reshape(512, 512)
        acc[...] += dot(gf[j], block)
        return 0

    lax.fori_loop(0, CHAN, multiply, 0)
    mix = acc[...].T
    out1.reshape(WIDTH, SEQ)[...] = (mix * gate[...].astype(F32)).astype(BF16)
    gg_ref[...] = (mix * conv[...].astype(F32)).astype(BF16)

    def exchange(src, dst, recv, sent):
        own = pltpu.make_async_copy(src.at[me], dst.at[me], local.at[2])
        own.start()

        def body(m, _):
            away = 16 - (m + 1) // 2
            there = lax.rem(z + ZN + away * (2 * lax.rem(m, 2) - 1), ZN)

            def go(flip_x, flip_core):
                peer = seq_index(x + flip_x * (1 - 2 * x), there, core + flip_core * (1 - 2 * core))
                pltpu.make_async_remote_copy(
                    src_ref=src.at[peer], dst_ref=dst.at[me], send_sem=sent, recv_sem=recv,
                    device_id={"seq": peer}, device_id_type=MESH,
                ).start()

            go(1, 0)
            go(1, 1)
            go(0, 1)

            @pl.when(m < ZN - 1)
            def _():
                go(0, 0)

            return 0

        lax.fori_loop(0, ZN, body, 0)
        own.wait()
        most = dst.at[pl.ds(0, SEQ - 1)]
        arrived(most, recv)
        return lambda: arrived(most, sent)

    finish_1 = exchange(out1, in1, recv_1, sent_1)

    outer_inner(dot(perm[...], in1.reshape(WIDTH, SEQ)[...]).astype(BF16))
    ours = wide_dot(turned[...], t2h[...], t2l[...])
    a_re, a_im = ours[:, :SEQ], ours[:, SEQ:]
    k_re, k_im = spec[:, :SEQ], spec[:, SEQ:]
    joined = jnp.concatenate([k_re * a_re + k_im * a_im, k_im * a_re - k_re * a_im], axis=1)
    deep = wide_dot(joined, t2h[...], t2l[...])
    parts = []
    for c in range(CH):
        re, im = deep[c * ROWS:(c + 1) * ROWS, :SEQ], deep[c * ROWS:(c + 1) * ROWS, SEQ:]
        parts.append(jnp.concatenate([re * twc[...] - im * tws[...], -(im * twc[...] + re * tws[...])], axis=0))
    full = dot_wide(t4h[...], t4l[...], jnp.concatenate(parts, axis=1)).astype(BF16)
    stacked = jnp.concatenate([full[:, c * SEQ:(c + 1) * SEQ] for c in range(CH)], axis=0)
    out2.reshape(WIDTH, SEQ)[...] = dot(back[...], stacked).astype(BF16)

    finish_2 = exchange(out2, in2, recv_2, sent_2)
    inner = in2.reshape(WIDTH, SEQ)[...].astype(F32)
    gk_ref[...] = (inner * value[...].astype(F32)).astype(BF16)
    gv_ref[...] = (inner * key[...].astype(F32)).astype(BF16)

    finish_1()
    finish_2()
    arrived(quarter, send_q)
    arrived(gf.at[pl.ds(0, 7)], send_g)
    for amount in (quarter, quarter, wf.at[x, pl.ds(0, 31), core]):
        arrived(amount, send_w)


def tables():
    total = 2 * SEQ * SEQ
    kept = np.arange(ROWS)
    used = kept <= SEQ
    block, tau = np.arange(SEQ), np.arange(SEQ)
    outer = 2 * np.pi * (np.outer(kept, block) % (2 * SEQ)) / (2 * SEQ)
    cos, sin = np.cos(outer) * used[:, None], -np.sin(outer) * used[:, None]
    twist = 2 * np.pi * np.outer(kept, tau) / total
    inner = 2 * np.pi * (np.outer(tau, tau) % SEQ) / SEQ
    c, s = np.cos(inner), -np.sin(inner)
    weight = np.where((kept == 0) | (kept == SEQ), 1.0, 2.0)[:, None] / total
    first = np.concatenate([cos, sin], axis=0)
    second = np.block([[c, s], [-s, c]])
    fourth = np.concatenate([cos * weight, sin * weight], axis=0).T

    def pair(v):
        v = v.astype(np.float32)
        high = v.astype(ml_dtypes.bfloat16)
        return high, (v - high.astype(np.float32)).astype(ml_dtypes.bfloat16)

    return (*pair(first), np.cos(twist).astype(np.float32), (-np.sin(twist)).astype(np.float32), *pair(second), *pair(fourth))


def per_device(grad_out, out_weight, gate_stream, conv_output, key_stream, value_stream, long_filter):
    filters = jnp.swapaxes(long_filter.reshape(CH, SEQ, SEQ), 0, 1)
    consts = [jnp.asarray(t) for t in tables()]
    space, anywhere = pl.BlockSpec(memory_space=VMEM), pl.BlockSpec(memory_space=pl.ANY)
    dma = pltpu.SemaphoreType.DMA
    stream = jax.ShapeDtypeStruct((WIDTH, SEQ), BF16)
    streams = [VMEM((WIDTH, SEQ), BF16)] * 4
    blocks = VMEM((SEQ, CH, SEQ), BF16)
    return pl.pallas_call(
        kernel,
        out_shape=(stream, stream, stream),
        in_specs=[anywhere] * 15,
        out_specs=(space, space, space),
        scratch_shapes=[
            VMEM((2, ZN, 2, 32, 512), BF16), VMEM((CHAN, SEQ, 512), BF16), VMEM((SEQ, 512), F32),
            *streams, blocks,
            *[VMEM(t.shape, t.dtype) for t in consts],
            VMEM((WIDTH, WIDTH), BF16), VMEM((WIDTH, WIDTH), BF16),
            VMEM((CH * ROWS, 2 * SEQ), F32), VMEM((CH * ROWS, 2 * SEQ), F32),
            blocks, blocks, blocks, blocks,
            dma((16,)), dma((16,)), dma, dma, dma, dma, dma, dma, dma, dma,
            dma, dma, dma, dma, dma((3,)), dma((13,)),
        ],
        compiler_params=pltpu.CompilerParams(collective_id=0, has_side_effects=True, vmem_limit_bytes=48 << 20),
        name="hyena_backward",
    )(grad_out, out_weight, gate_stream, conv_output, key_stream, value_stream, filters, *consts)


def solution(mesh):
    in_specs = (
        P("seq", "chan"), P("seq", "chan"), P("chan", "seq"), P("chan", "seq"),
        P("chan", "seq"), P("chan", "seq"), P(("chan", "seq"), None),
    )
    out_specs = (P("chan", "seq"), P("chan", "seq"), P("chan", "seq"))
    return jax.shard_map(per_device, mesh=mesh, in_specs=in_specs, out_specs=out_specs, check_vma=False)
```

```python
import jax
import jax.numpy as jnp
import ml_dtypes
import numpy as np
from jax import lax
from jax.experimental import pallas as pl
from jax.experimental.pallas import tpu as pltpu
from jax.sharding import PartitionSpec as P

MESH = pl.DeviceIdType.MESH
VMEM = pltpu.VMEM
F32 = jnp.float32
BF16 = jnp.bfloat16
ZN = 32
CHAN = 8
SEQ = 128
CH = 4
ROWS = 144
JUMP = 3
GROUPS = 5
LAG = 3
WIDTH = SEQ * CH


def seq_index(x, z, core):
    return (x * ZN + z) * 2 + core


def split(values):
    high = values.astype(BF16)
    return high, (values - high.astype(F32)).astype(BF16)


def dot(a, b):
    return jnp.dot(a, b, preferred_element_type=F32)


def wide_dot(values, high, low):
    a, b = split(values)
    return dot(a, high) + (dot(b, high) + dot(a, low))


def dot_wide(high, low, values):
    a, b = split(values)
    return dot(high, a) + (dot(high, b) + dot(low, a))


def kernel(g_hbm, w_hbm, gate_hbm, conv_hbm, key_hbm, value_hbm, filt_hbm,
           t1h_hbm, t1l_hbm, twc_hbm, tws_hbm, t2h_hbm, t2l_hbm, t4h_hbm, t4l_hbm,
           gg_ref, gk_ref, gv_ref,
           wf, gf, acc, gate, conv, key, value, filt,
           t1h, t1l, twc, tws, t2h, t2l, t4h, t4l,
           perm, back, turned, spec, out1, in1, out2, in2,
           recv_r, recv_l, recv_x, recv_p, recv_q, recv_gx, recv_gy, send_w, send_q, send_g,
           recv_1, sent_1, recv_2, sent_2, local, loads):
    me = lax.axis_index("seq")
    chan = lax.axis_index("chan")
    x, z, core = me // (2 * ZN), lax.rem(me // 2, ZN), lax.rem(me, 2)
    def along(step):
        return seq_index(x, lax.rem(z + ZN + step, ZN), core)

    partner, across = seq_index(x, z, 1 - core), seq_index(1 - x, z, core)
    y, x_hi = chan // 2, lax.rem(chan, 2)
    opposite = y * 2 + 1 - x_hi
    rows = [lax.rem(y + step, 4) * 2 + x_hi for step in (1, 3, 2)]

    barrier = pltpu.get_barrier_semaphore()
    for peer in (along(1), along(-1), along(JUMP), along(-JUMP), partner, across):
        pl.semaphore_signal(barrier, inc=1, device_id={"seq": peer}, device_id_type=MESH)
    for peer in (opposite, *rows):
        pl.semaphore_signal(barrier, inc=1, device_id={"chan": peer}, device_id_type=MESH)
    own_w = pltpu.make_async_copy(w_hbm, wf.at[x, z, core], local.at[0])
    own_g = pltpu.make_async_copy(g_hbm, gf.at[chan], local.at[1])
    own_w.start()
    own_g.start()
    early = [(filt_hbm, filt), (t1h_hbm, t1h), (t1l_hbm, t1l), (twc_hbm, twc), (tws_hbm, tws), (t2h_hbm, t2h), (t2l_hbm, t2l)]
    late = [(gate_hbm, gate), (conv_hbm, conv), (key_hbm, key), (value_hbm, value), (t4h_hbm, t4h), (t4l_hbm, t4l)]
    pulls = [pltpu.make_async_copy(src, dst, loads.at[n]) for n, (src, dst) in enumerate(early + late)]
    for pull in pulls:
        pull.start()
    pl.semaphore_wait(barrier, 10)

    def send(src, slot_x, slot_z, target, send_sem, recv_sem):
        pltpu.make_async_remote_copy(
            src_ref=src, dst_ref=wf.at[slot_x, slot_z, core], send_sem=send_sem, recv_sem=recv_sem,
            device_id={"seq": target}, device_id_type=MESH,
        ).start()

    def send_g_to(src, slot, target, recv_sem):
        pltpu.make_async_remote_copy(
            src_ref=src, dst_ref=gf.at[slot], send_sem=send_g, recv_sem=recv_sem,
            device_id={"chan": target}, device_id_type=MESH,
        ).start()

    for step in (JUMP, 1):
        send(w_hbm, x, z, along(step), send_w, recv_r.at[step])
        send(w_hbm, x, z, along(-step), send_w, recv_l.at[step])
    send(w_hbm, x, z, across, send_w, recv_x.at[GROUPS])
    send(w_hbm, x, z, partner, send_w, recv_p)
    send_g_to(g_hbm, chan, opposite, recv_gx)
    for peer in rows:
        send_g_to(g_hbm, chan, peer, recv_gy)

    def arrived(here, sem):
        pltpu.make_async_copy(here, here, sem).wait()

    def outer_inner(blocks):
        beside = jnp.concatenate([blocks[c * SEQ:(c + 1) * SEQ] for c in range(CH)], axis=1)
        part = dot(t1h[...], beside) + dot(t1l[...], beside)
        for c in range(CH):
            re, im = part[:ROWS, c * SEQ:(c + 1) * SEQ], part[ROWS:, c * SEQ:(c + 1) * SEQ]
            turned[c * ROWS:(c + 1) * ROWS, :SEQ] = re * twc[...] - im * tws[...]
            turned[c * ROWS:(c + 1) * ROWS, SEQ:] = re * tws[...] + im * twc[...]

    def slot(sign, away):
        return lax.rem(z + 2 * ZN - sign * away, ZN)

    def land(sign, away):
        arrived(wf.at[x, slot(sign, away), core], (recv_r if sign > 0 else recv_l).at[away])

    def relay(sign, away, step):
        source = slot(sign, away)
        send(wf.at[x, source, core], x, source, along(sign * step), send_w, (recv_r if sign > 0 else recv_l).at[away + step])

    def spread(sign, away, group):
        source = slot(sign, away)
        shard = wf.at[x, source, core]
        send(shard, x, source, across, send_w, recv_x.at[group])
        send(shard, x, source, partner, send_w, recv_p)

    def hand_over(sign, away):
        source = slot(sign, away)
        send(wf.at[1 - x, source, core], 1 - x, source, partner, send_q, recv_q)

    def hand_over_group(group):
        arrived(wf.at[1 - x, pl.ds(0, 2 * JUMP), core], recv_x.at[group])
        for away in range(1, JUMP + 1):
            hand_over(1, JUMP * group + away)
            hand_over(-1, JUMP * group + away)

    def prepare(group):
        @pl.when(group == 0)
        def _():
            arrived(gf.at[opposite], recv_gx)
            for peer in rows:
                send_g_to(gf.at[opposite], opposite, peer, recv_gy)

        @pl.when(group == 1)
        def _():
            row = lax.broadcasted_iota(jnp.int32, (WIDTH, WIDTH), 0)
            col = lax.broadcasted_iota(jnp.int32, (WIDTH, WIDTH), 1)
            perm[...] = jnp.where(col == ((row & (SEQ - 1)) << 2 | row >> 7), 1.0, 0.0).astype(BF16)
            back[...] = jnp.where(col == ((row & (CH - 1)) << 7 | row >> 2), 1.0, 0.0).astype(BF16)
            for pull in pulls[:len(early)]:
                pull.wait()

        @pl.when(group == 2)
        def _():
            outer_inner(dot(perm[...], filt.reshape(WIDTH, SEQ)[...]).astype(BF16))

        @pl.when(group == 3)
        def _():
            spec[...] = wide_dot(turned[...], t2h[...], t2l[...])

    def advance(group, _):
        near, middle, far = JUMP * group + 1, JUMP * group + 2, JUMP * group + 3
        for sign in (1, -1):
            land(sign, near)
            relay(sign, near, 1)
        for sign in (1, -1):
            land(sign, far)

            @pl.when(group < GROUPS - 1)
            def _():
                relay(sign, far, JUMP)
                relay(sign, far, 1)

        for sign in (1, -1):
            spread(sign, near, group)
            spread(sign, far, group)

        @pl.when(group == GROUPS - 1)
        def _():
            relay(1, far, 1)

        prepare(group)
        for sign in (1, -1):
            land(sign, middle)
            spread(sign, middle, group)

        @pl.when(group >= LAG)
        def _():
            hand_over_group(group - LAG)

        return 0

    lax.fori_loop(0, GROUPS, advance, 0)
    land(1, 16)
    spread(1, 16, GROUPS)
    lax.fori_loop(GROUPS - LAG, GROUPS, lambda group, _: (hand_over_group(group), 0)[1], 0)
    arrived(wf.at[1 - x, pl.ds(0, 2), core], recv_x.at[GROUPS])
    hand_over(1, 0)
    hand_over(1, 16)
    quarter = wf.at[1 - x, :, core]

    own_w.wait()
    own_g.wait()
    for pull in pulls[len(early):]:
        pull.wait()
    arrived(gf.at[pl.ds(0, 6)], recv_gy)
    arrived(wf.at[x, :, 1 - core], recv_p)
    arrived(wf.at[1 - x, :, 1 - core], recv_q)

    acc[...] = jnp.zeros_like(acc)

    def multiply(j, _):
        block = wf[j // 4, pl.ds(lax.rem(j, 4) * 8, 8)].reshape(512, 512)
        acc[...] += dot(gf[j], block)
        return 0

    lax.fori_loop(0, CHAN, multiply, 0)
    mix = acc[...].T
    out1.reshape(WIDTH, SEQ)[...] = (mix * gate[...].astype(F32)).astype(BF16)
    gg_ref[...] = (mix * conv[...].astype(F32)).astype(BF16)

    def exchange(src, dst, recv, sent):
        own = pltpu.make_async_copy(src.at[me], dst.at[me], local.at[2])
        own.start()

        def body(m, _):
            away = 16 - (m + 1) // 2
            there = lax.rem(z + ZN + away * (2 * lax.rem(m, 2) - 1), ZN)

            def go(flip_x, flip_core):
                peer = seq_index(x + flip_x * (1 - 2 * x), there, core + flip_core * (1 - 2 * core))
                pltpu.make_async_remote_copy(
                    src_ref=src.at[peer], dst_ref=dst.at[me], send_sem=sent, recv_sem=recv,
                    device_id={"seq": peer}, device_id_type=MESH,
                ).start()

            go(1, 0)
            go(1, 1)
            go(0, 1)

            @pl.when(m < ZN - 1)
            def _():
                go(0, 0)

            return 0

        lax.fori_loop(0, ZN, body, 0)
        own.wait()
        most = dst.at[pl.ds(0, SEQ - 1)]
        arrived(most, recv)
        return lambda: arrived(most, sent)

    finish_1 = exchange(out1, in1, recv_1, sent_1)

    outer_inner(dot(perm[...], in1.reshape(WIDTH, SEQ)[...]).astype(BF16))
    ours = wide_dot(turned[...], t2h[...], t2l[...])
    a_re, a_im = ours[:, :SEQ], ours[:, SEQ:]
    k_re, k_im = spec[:, :SEQ], spec[:, SEQ:]
    joined = jnp.concatenate([k_re * a_re + k_im * a_im, k_im * a_re - k_re * a_im], axis=1)
    deep = wide_dot(joined, t2h[...], t2l[...])
    parts = []
    for c in range(CH):
        re, im = deep[c * ROWS:(c + 1) * ROWS, :SEQ], deep[c * ROWS:(c + 1) * ROWS, SEQ:]
        parts.append(jnp.concatenate([re * twc[...] - im * tws[...], -(im * twc[...] + re * tws[...])], axis=0))
    full = dot_wide(t4h[...], t4l[...], jnp.concatenate(parts, axis=1)).astype(BF16)
    stacked = jnp.concatenate([full[:, c * SEQ:(c + 1) * SEQ] for c in range(CH)], axis=0)
    out2.reshape(WIDTH, SEQ)[...] = dot(back[...], stacked).astype(BF16)

    finish_2 = exchange(out2, in2, recv_2, sent_2)
    inner = in2.reshape(WIDTH, SEQ)[...].astype(F32)
    gk_ref[...] = (inner * value[...].astype(F32)).astype(BF16)
    gv_ref[...] = (inner * key[...].astype(F32)).astype(BF16)

    finish_1()
    finish_2()
    arrived(quarter, send_q)
    arrived(gf.at[pl.ds(0, 7)], send_g)
    for amount in (quarter, quarter, wf.at[x, pl.ds(0, 31), core]):
        arrived(amount, send_w)


def tables():
    total = 2 * SEQ * SEQ
    kept = np.arange(ROWS)
    used = kept <= SEQ
    block, tau = np.arange(SEQ), np.arange(SEQ)
    outer = 2 * np.pi * (np.outer(kept, block) % (2 * SEQ)) / (2 * SEQ)
    cos, sin = np.cos(outer) * used[:, None], -np.sin(outer) * used[:, None]
    twist = 2 * np.pi * np.outer(kept, tau) / total
    inner = 2 * np.pi * (np.outer(tau, tau) % SEQ) / SEQ
    c, s = np.cos(inner), -np.sin(inner)
    weight = np.where((kept == 0) | (kept == SEQ), 1.0, 2.0)[:, None] / total
    first = np.concatenate([cos, sin], axis=0)
    second = np.block([[c, s], [-s, c]])
    fourth = np.concatenate([cos * weight, sin * weight], axis=0).T

    def pair(v):
        v = v.astype(np.float32)
        high = v.astype(ml_dtypes.bfloat16)
        return high, (v - high.astype(np.float32)).astype(ml_dtypes.bfloat16)

    return (*pair(first), np.cos(twist).astype(np.float32), (-np.sin(twist)).astype(np.float32), *pair(second), *pair(fourth))


def per_device(grad_out, out_weight, gate_stream, conv_output, key_stream, value_stream, long_filter):
    filters = jnp.swapaxes(long_filter.reshape(CH, SEQ, SEQ), 0, 1)
    consts = [jnp.asarray(t) for t in tables()]
    space, anywhere = pl.BlockSpec(memory_space=VMEM), pl.BlockSpec(memory_space=pltpu.HBM)
    dma = pltpu.SemaphoreType.DMA
    stream = jax.ShapeDtypeStruct((WIDTH, SEQ), BF16)
    streams = [VMEM((WIDTH, SEQ), BF16)] * 4
    blocks = VMEM((SEQ, CH, SEQ), BF16)
    return pl.pallas_call(
        kernel,
        out_shape=(stream, stream, stream),
        in_specs=[anywhere] * 15,
        out_specs=(space, space, space),
        scratch_shapes=[
            VMEM((2, ZN, 2, 32, 512), BF16), VMEM((CHAN, SEQ, 512), BF16), VMEM((SEQ, 512), F32),
            *streams, blocks,
            *[VMEM(t.shape, t.dtype) for t in consts],
            VMEM((WIDTH, WIDTH), BF16), VMEM((WIDTH, WIDTH), BF16),
            VMEM((CH * ROWS, 2 * SEQ), F32), VMEM((CH * ROWS, 2 * SEQ), F32),
            blocks, blocks, blocks, blocks,
            dma((17,)), dma((16,)), dma((GROUPS + 1,)), dma, dma, dma, dma, dma, dma, dma,
            dma, dma, dma, dma, dma((3,)), dma((13,)),
        ],
        compiler_params=pltpu.CompilerParams(collective_id=0, has_side_effects=True),
        name="hyena_backward",
    )(grad_out, out_weight, gate_stream, conv_output, key_stream, value_stream, filters, *consts)


def solution(mesh):
    in_specs = (
        P("seq", "chan"), P("seq", "chan"), P("chan", "seq"), P("chan", "seq"),
        P("chan", "seq"), P("chan", "seq"), P(("chan", "seq"), None),
    )
    out_specs = (P("chan", "seq"), P("chan", "seq"), P("chan", "seq"))
    return jax.shard_map(per_device, mesh=mesh, in_specs=in_specs, out_specs=out_specs, check_vma=False)
```

```python
import jax
import jax.numpy as jnp
import ml_dtypes
import numpy as np
from jax import lax
from jax.experimental import pallas as pl
from jax.experimental.pallas import tpu as pltpu
from jax.sharding import PartitionSpec as P

MESH = pl.DeviceIdType.MESH
VMEM = pltpu.VMEM
F32 = jnp.float32
BF16 = jnp.bfloat16
ZN = 32
CHAN = 8
SEQ = 128
CH = 4
ROWS = 144
JUMP = 3
GROUPS = 5
LAG = 3
WIDTH = SEQ * CH


def seq_index(x, z, core):
    return (x * ZN + z) * 2 + core


def split(values):
    high = values.astype(BF16)
    return high, (values - high.astype(F32)).astype(BF16)


def dot(a, b):
    return jnp.dot(a, b, preferred_element_type=F32)


def wide_dot(values, high, low):
    a, b = split(values)
    return dot(a, high) + (dot(b, high) + dot(a, low))


def dot_wide(high, low, values):
    a, b = split(values)
    return dot(high, a) + (dot(high, b) + dot(low, a))


def kernel(g_hbm, w_hbm, gate_hbm, conv_hbm, key_hbm, value_hbm, filt_hbm,
           t1h_hbm, t1l_hbm, twc_hbm, tws_hbm, t2h_hbm, t2l_hbm, t4h_hbm, t4l_hbm,
           grads,
           wf, gf, acc, gate, conv, key, value, filt,
           t1h, t1l, twc, tws, t2h, t2l, t4h, t4l,
           perm, back, turned, spec, out1, in1, out2, in2,
           recv_r, recv_l, recv_x, recv_p, recv_q, recv_gx, recv_gy, send_w, send_q, send_g,
           recv_1, sent_1, recv_2, sent_2, local, loads):
    me = lax.axis_index("seq")
    chan = lax.axis_index("chan")
    x, z, core = me // (2 * ZN), lax.rem(me // 2, ZN), lax.rem(me, 2)
    def along(step):
        return seq_index(x, lax.rem(z + ZN + step, ZN), core)

    partner, across = seq_index(x, z, 1 - core), seq_index(1 - x, z, core)
    y, x_hi = chan // 2, lax.rem(chan, 2)
    opposite = y * 2 + 1 - x_hi
    rows = [lax.rem(y + step, 4) * 2 + x_hi for step in (1, 3, 2)]

    barrier = pltpu.get_barrier_semaphore()
    for peer in (along(1), along(-1), along(JUMP), along(-JUMP), partner, across):
        pl.semaphore_signal(barrier, inc=1, device_id={"seq": peer}, device_id_type=MESH)
    for peer in (opposite, *rows):
        pl.semaphore_signal(barrier, inc=1, device_id={"chan": peer}, device_id_type=MESH)
    own_w = pltpu.make_async_copy(w_hbm, wf.at[x, z, core], local.at[0])
    own_g = pltpu.make_async_copy(g_hbm, gf.at[chan], local.at[1])
    own_w.start()
    own_g.start()
    early = [(filt_hbm, filt), (t1h_hbm, t1h), (t1l_hbm, t1l), (twc_hbm, twc), (tws_hbm, tws), (t2h_hbm, t2h), (t2l_hbm, t2l)]
    late = [(gate_hbm, gate), (conv_hbm, conv), (key_hbm, key), (value_hbm, value), (t4h_hbm, t4h), (t4l_hbm, t4l)]
    pulls = [pltpu.make_async_copy(src, dst, loads.at[n]) for n, (src, dst) in enumerate(early + late)]
    for pull in pulls:
        pull.start()
    pl.semaphore_wait(barrier, 10)

    def send(src, slot_x, slot_z, target, send_sem, recv_sem):
        pltpu.make_async_remote_copy(
            src_ref=src, dst_ref=wf.at[slot_x, slot_z, core], send_sem=send_sem, recv_sem=recv_sem,
            device_id={"seq": target}, device_id_type=MESH,
        ).start()

    def send_g_to(src, slot, target, recv_sem):
        pltpu.make_async_remote_copy(
            src_ref=src, dst_ref=gf.at[slot], send_sem=send_g, recv_sem=recv_sem,
            device_id={"chan": target}, device_id_type=MESH,
        ).start()

    for step in (JUMP, 1):
        send(w_hbm, x, z, along(step), send_w, recv_r.at[step])
        send(w_hbm, x, z, along(-step), send_w, recv_l.at[step])
    send(w_hbm, x, z, across, send_w, recv_x.at[GROUPS])
    send(w_hbm, x, z, partner, send_w, recv_p)
    send_g_to(g_hbm, chan, opposite, recv_gx)
    for peer in rows:
        send_g_to(g_hbm, chan, peer, recv_gy)

    def arrived(here, sem):
        pltpu.make_async_copy(here, here, sem).wait()

    def outer_inner(blocks):
        beside = jnp.concatenate([blocks[c * SEQ:(c + 1) * SEQ] for c in range(CH)], axis=1)
        part = dot(t1h[...], beside) + dot(t1l[...], beside)
        for c in range(CH):
            re, im = part[:ROWS, c * SEQ:(c + 1) * SEQ], part[ROWS:, c * SEQ:(c + 1) * SEQ]
            turned[c * ROWS:(c + 1) * ROWS, :SEQ] = re * twc[...] - im * tws[...]
            turned[c * ROWS:(c + 1) * ROWS, SEQ:] = re * tws[...] + im * twc[...]

    def slot(sign, away):
        return lax.rem(z + 2 * ZN - sign * away, ZN)

    def land(sign, away):
        arrived(wf.at[x, slot(sign, away), core], (recv_r if sign > 0 else recv_l).at[away])

    def relay(sign, away, step):
        source = slot(sign, away)
        send(wf.at[x, source, core], x, source, along(sign * step), send_w, (recv_r if sign > 0 else recv_l).at[away + step])

    def spread(sign, away, group):
        source = slot(sign, away)
        shard = wf.at[x, source, core]
        send(shard, x, source, across, send_w, recv_x.at[group])
        send(shard, x, source, partner, send_w, recv_p)

    def hand_over(sign, away):
        source = slot(sign, away)
        send(wf.at[1 - x, source, core], 1 - x, source, partner, send_q, recv_q)

    def hand_over_group(group):
        arrived(wf.at[1 - x, pl.ds(0, 2 * JUMP), core], recv_x.at[group])
        for away in range(1, JUMP + 1):
            hand_over(1, JUMP * group + away)
            hand_over(-1, JUMP * group + away)

    def prepare(group):
        @pl.when(group == 0)
        def _():
            arrived(gf.at[opposite], recv_gx)
            for peer in rows:
                send_g_to(gf.at[opposite], opposite, peer, recv_gy)

        @pl.when(group == 1)
        def _():
            row = lax.broadcasted_iota(jnp.int32, (WIDTH, WIDTH), 0)
            col = lax.broadcasted_iota(jnp.int32, (WIDTH, WIDTH), 1)
            perm[...] = jnp.where(col == ((row & (SEQ - 1)) << 2 | row >> 7), 1.0, 0.0).astype(BF16)
            back[...] = jnp.where(col == ((row & (CH - 1)) << 7 | row >> 2), 1.0, 0.0).astype(BF16)
            for pull in pulls[:len(early)]:
                pull.wait()

        @pl.when(group == 2)
        def _():
            outer_inner(dot(perm[...], filt.reshape(WIDTH, SEQ)[...]).astype(BF16))

        @pl.when(group == 3)
        def _():
            spec[...] = wide_dot(turned[...], t2h[...], t2l[...])

    def advance(group, _):
        near, middle, far = JUMP * group + 1, JUMP * group + 2, JUMP * group + 3
        for sign in (1, -1):
            land(sign, near)
            relay(sign, near, 1)
        for sign in (1, -1):
            land(sign, far)

            @pl.when(group < GROUPS - 1)
            def _():
                relay(sign, far, JUMP)
                relay(sign, far, 1)

        for sign in (1, -1):
            spread(sign, near, group)
            spread(sign, far, group)

        @pl.when(group == GROUPS - 1)
        def _():
            relay(1, far, 1)

        prepare(group)
        for sign in (1, -1):
            land(sign, middle)
            spread(sign, middle, group)

        @pl.when(group >= LAG)
        def _():
            hand_over_group(group - LAG)

        return 0

    lax.fori_loop(0, GROUPS, advance, 0)
    land(1, 16)
    spread(1, 16, GROUPS)
    lax.fori_loop(GROUPS - LAG, GROUPS - 1, lambda group, _: (hand_over_group(group), 0)[1], 0)
    own_w.wait()
    own_g.wait()
    for pull in pulls[len(early):]:
        pull.wait()
    acc[...] = jnp.zeros_like(acc)
    arrived(gf.at[pl.ds(0, 6)], recv_gy)

    def multiply(side):
        def body(j, _):
            block = wf[side, pl.ds(j * 8, 8)].reshape(512, 512)
            acc[...] += dot(gf[side * 4 + j], block)
            return 0

        lax.fori_loop(0, 4, body, 0)

    arrived(wf.at[x, :, 1 - core], recv_p)
    multiply(x)
    hand_over_group(GROUPS - 1)
    arrived(wf.at[1 - x, pl.ds(0, 2), core], recv_x.at[GROUPS])
    hand_over(1, 0)
    hand_over(1, 16)
    quarter = wf.at[1 - x, :, core]
    arrived(wf.at[1 - x, :, 1 - core], recv_q)
    multiply(1 - x)
    mix = acc[...].T
    out1.reshape(WIDTH, SEQ)[...] = (mix * gate[...].astype(F32)).astype(BF16)
    grads[0] = (mix * conv[...].astype(F32)).astype(BF16)

    def exchange(src, dst, recv, sent):
        own = pltpu.make_async_copy(src.at[me], dst.at[me], local.at[2])
        own.start()

        def body(m, _):
            away = 16 - (m + 1) // 2
            there = lax.rem(z + ZN + away * (2 * lax.rem(m, 2) - 1), ZN)

            def go(flip_x, flip_core):
                peer = seq_index(x + flip_x * (1 - 2 * x), there, core + flip_core * (1 - 2 * core))
                pltpu.make_async_remote_copy(
                    src_ref=src.at[peer], dst_ref=dst.at[me], send_sem=sent, recv_sem=recv,
                    device_id={"seq": peer}, device_id_type=MESH,
                ).start()

            go(1, 0)
            go(1, 1)
            go(0, 1)

            @pl.when(m < ZN - 1)
            def _():
                go(0, 0)

            return 0

        lax.fori_loop(0, ZN, body, 0)
        own.wait()
        most = dst.at[pl.ds(0, SEQ - 1)]
        arrived(most, recv)
        return lambda: arrived(most, sent)

    finish_1 = exchange(out1, in1, recv_1, sent_1)

    outer_inner(dot(perm[...], in1.reshape(WIDTH, SEQ)[...]).astype(BF16))
    ours = wide_dot(turned[...], t2h[...], t2l[...])
    a_re, a_im = ours[:, :SEQ], ours[:, SEQ:]
    k_re, k_im = spec[:, :SEQ], spec[:, SEQ:]
    joined = jnp.concatenate([k_re * a_re + k_im * a_im, k_im * a_re - k_re * a_im], axis=1)
    deep = wide_dot(joined, t2h[...], t2l[...])
    parts = []
    for c in range(CH):
        re, im = deep[c * ROWS:(c + 1) * ROWS, :SEQ], deep[c * ROWS:(c + 1) * ROWS, SEQ:]
        parts.append(jnp.concatenate([re * twc[...] - im * tws[...], -(im * twc[...] + re * tws[...])], axis=0))
    full = dot_wide(t4h[...], t4l[...], jnp.concatenate(parts, axis=1)).astype(BF16)
    stacked = jnp.concatenate([full[:, c * SEQ:(c + 1) * SEQ] for c in range(CH)], axis=0)
    out2.reshape(WIDTH, SEQ)[...] = dot(back[...], stacked).astype(BF16)

    finish_2 = exchange(out2, in2, recv_2, sent_2)
    inner = in2.reshape(WIDTH, SEQ)[...].astype(F32)
    grads[1] = (inner * value[...].astype(F32)).astype(BF16)
    grads[2] = (inner * key[...].astype(F32)).astype(BF16)

    finish_1()
    finish_2()
    arrived(quarter, send_q)
    arrived(gf.at[pl.ds(0, 7)], send_g)
    for amount in (quarter, quarter, wf.at[x, pl.ds(0, 31), core]):
        arrived(amount, send_w)


def tables():
    total = 2 * SEQ * SEQ
    kept = np.arange(ROWS)
    used = kept <= SEQ
    block, tau = np.arange(SEQ), np.arange(SEQ)
    outer = 2 * np.pi * (np.outer(kept, block) % (2 * SEQ)) / (2 * SEQ)
    cos, sin = np.cos(outer) * used[:, None], -np.sin(outer) * used[:, None]
    twist = 2 * np.pi * np.outer(kept, tau) / total
    inner = 2 * np.pi * (np.outer(tau, tau) % SEQ) / SEQ
    c, s = np.cos(inner), -np.sin(inner)
    weight = np.where((kept == 0) | (kept == SEQ), 1.0, 2.0)[:, None] / total
    first = np.concatenate([cos, sin], axis=0)
    second = np.block([[c, s], [-s, c]])
    fourth = np.concatenate([cos * weight, sin * weight], axis=0).T

    def pair(v):
        v = v.astype(np.float32)
        high = v.astype(ml_dtypes.bfloat16)
        return high, (v - high.astype(np.float32)).astype(ml_dtypes.bfloat16)

    return (*pair(first), np.cos(twist).astype(np.float32), (-np.sin(twist)).astype(np.float32), *pair(second), *pair(fourth))


def per_device(grad_out, out_weight, gate_stream, conv_output, key_stream, value_stream, long_filter):
    filters = jnp.swapaxes(long_filter.reshape(CH, SEQ, SEQ), 0, 1)
    consts = [jnp.asarray(t) for t in tables()]
    space, anywhere = pl.BlockSpec(memory_space=VMEM), pl.BlockSpec(memory_space=pltpu.HBM)
    dma = pltpu.SemaphoreType.DMA
    streams = [VMEM((WIDTH, SEQ), BF16)] * 4
    blocks = VMEM((SEQ, CH, SEQ), BF16)
    grads = pl.pallas_call(
        kernel,
        out_shape=jax.ShapeDtypeStruct((3, WIDTH, SEQ), BF16),
        in_specs=[anywhere] * 15,
        out_specs=space,
        scratch_shapes=[
            VMEM((2, ZN, 2, 32, 512), BF16), VMEM((CHAN, SEQ, 512), BF16), VMEM((SEQ, 512), F32),
            *streams, blocks,
            *[VMEM(t.shape, t.dtype) for t in consts],
            VMEM((WIDTH, WIDTH), BF16), VMEM((WIDTH, WIDTH), BF16),
            VMEM((CH * ROWS, 2 * SEQ), F32), VMEM((CH * ROWS, 2 * SEQ), F32),
            blocks, blocks, blocks, blocks,
            dma((17,)), dma((16,)), dma((GROUPS + 1,)), dma, dma, dma, dma, dma, dma, dma,
            dma, dma, dma, dma, dma((3,)), dma((13,)),
        ],
        compiler_params=pltpu.CompilerParams(collective_id=0, has_side_effects=True),
        name="hyena_backward",
    )(grad_out, out_weight, gate_stream, conv_output, key_stream, value_stream, filters, *consts)
    return (grads[0], grads[1], grads[2])


def solution(mesh):
    in_specs = (
        P("seq", "chan"), P("seq", "chan"), P("chan", "seq"), P("chan", "seq"),
        P("chan", "seq"), P("chan", "seq"), P(("chan", "seq"), None),
    )
    out_specs = (P("chan", "seq"), P("chan", "seq"), P("chan", "seq"))
    return jax.shard_map(per_device, mesh=mesh, in_specs=in_specs, out_specs=out_specs, check_vma=False)
```
